32 devices in a mesh: band: 4 (over z), grid: 8 (over y, x, core).
Axes of the slice: x: 2, y: 2, z: 4, core: 2. Of those that a mesh axis runs over, the one named last changes fastest.
Arguments:
- orbitals: bfloat16 [8, 256, 256, 256], P('band', 'grid'), may hold values from -60 to 60
- potential: float32 [256, 256, 256], P('grid'), may hold values from -2 to 1
Outputs:
- rotated: bfloat16 [8, 256, 256, 256], P('band', 'grid')
- projected: float32 [8, 8], replicated
The draws below stay inside these ranges and needn't reach their ends.
All inputs are finite; a program needn't handle non-finite values. Where the reference program divides by a largest or mean magnitude, that divisor is 1e-20 or more.
Results may differ from the reference program's by a relative error of at most 0.0005.
The reference program's roundings to bfloat16 on the way count: a program that leaves them out, or rounds other values in their place, can miss the bound.
Values may be sent and summed in bfloat16 or wider, within the bound.
A program may use at most 192 MiB of HBM per device.

```python
import math
import jax
import jax.numpy as jnp
from jax import lax

NX = 256
NY = 256
NZ = 256
NS_ITERS = 6
NB = 8


def draw_orbitals(key, part):
    key_base = jax.random.fold_in(key, 11)
    key_mix = jax.random.fold_in(key, 23)
    key_scale = jax.random.fold_in(key, 37)
    key_lines = jax.random.fold_in(key, 41)
    key_wave = jax.random.fold_in(key, 53)
    key_phase = jax.random.fold_in(key, 67)
    key_along_y = jax.random.fold_in(key, 79)
    key_along_z = jax.random.fold_in(key, 83)
    base = jnp.clip(jax.random.normal(key_base, (NB, NX * NY * NZ), jnp.float32), -4.0, 4.0)
    line_noise = jnp.clip(jax.random.normal(key_lines, (NB, 2, NY, NZ), jnp.float32), -4.0, 4.0)
    top = 3.0
    mixing = jnp.eye(NB, dtype=jnp.float32) + 0.5 * jax.random.normal(key_mix, (NB, NB), jnp.float32) / math.sqrt(NB)
    scales = jnp.exp(jax.random.uniform(key_scale, (NB,), jnp.float32, 0.0, math.log(3.2)))
    mixed = jnp.dot(mixing, base).reshape(NB, NX, NY, NZ)
    top_mode = max(NX // 32, 1)
    wave_number = jax.random.randint(key_wave, (NB, 2), 1, top_mode + 1).astype(jnp.float32)
    phases = jax.random.uniform(key_phase, (NB, 2), jnp.float32, 0.0, 2.0 * math.pi)
    plane_index = jnp.arange(NX, dtype=jnp.float32)
    wave_rows = jnp.cos(wave_number[:, :, None] * plane_index[None, None, :] * (2.0 * math.pi / NX) + phases[:, :, None])
    smooth = wave_rows[:, 0, :, None, None] * line_noise[:, 0, None, :, :] + wave_rows[:, 1, :, None, None] * line_noise[:, 1, None, :, :]
    along_y = jnp.exp(jax.random.uniform(key_along_y, (NY,), jnp.float32, math.log(0.6), math.log(1.7)))
    along_z = jnp.exp(jax.random.uniform(key_along_z, (NZ,), jnp.float32, math.log(0.6), math.log(1.7)))
    position = jnp.arange(NX, dtype=jnp.float32) / max(NX - 1, 1)
    envelope = 1.0 + (top - 1.0) * position
    values = 0.75 * (mixed + smooth) * scales[:, None, None, None] * envelope[None, :, None, None]
    values = values * along_y[None, None, :, None] * along_z[None, None, None, :]
    return jnp.clip(values, -60.0, 60.0).astype(jnp.bfloat16)


def level_of(own_key, extent, shards, least, top_value):
    def one(dim, blocks):
        draws = jax.random.uniform(jax.random.fold_in(jax.random.fold_in(own_key, 6), dim), (blocks,), jnp.float32, least / len(shards), top_value / len(shards))
        return jnp.repeat(jnp.exp(draws), extent[dim] // blocks).reshape((-1,) + (1,) * (len(extent) - dim - 1))

    level = one(*shards[0])
    for cut in shards[1:]:
        level = level * one(*cut)
    return level


def setup_inputs(seed: int = 0) -> dict:
    key_of = jax.random.split(jax.random.key(seed), 3)
    return {
        "orbitals": draw_orbitals(jax.random.fold_in(key_of[2], 71), 0),
        "potential": jnp.clip(-2.0 + 3.0 * jax.random.uniform(key_of[1], (NX, NY, NZ), jnp.float32) ** level_of(key_of[1], (NX, NY, NZ), ((0, 8),), -0.2, 0.2), -2.0, 1.0),
    }


CENTER = 9.5
HALF_WIDTH = 6.5


def second_derivative(length):
    index = jnp.arange(length, dtype=jnp.int32)
    product = (index[:, None] * index[None, :]) % length
    angles = product.astype(jnp.float32) * (2.0 * math.pi / length)
    freq = jnp.minimum(index, length - index).astype(jnp.float32)
    weight = -((2.0 * math.pi / length) * freq) ** 2 / length
    cosines = jnp.cos(angles)
    sines = jnp.sin(angles)
    matrix = jnp.dot(cosines * weight[None, :], cosines.T, precision=lax.Precision.HIGHEST)
    matrix = matrix + jnp.dot(sines * weight[None, :], sines.T, precision=lax.Precision.HIGHEST)
    return matrix.astype(jnp.bfloat16)


def apply_ham(field, potential, k_x, k_y, k_z):
    wide = field.astype(jnp.float32)
    term_z = jnp.dot(field.reshape(-1, NZ), k_z, preferred_element_type=jnp.float32).reshape(NX, NY, NZ)
    term_y = jnp.einsum('xjz,jy->xyz', wide, k_y.astype(jnp.float32))
    term_x = jnp.einsum('jyz,jx->xyz', wide, k_x.astype(jnp.float32)).astype(jnp.bfloat16)
    return -0.5 * (term_x.astype(jnp.float32) + term_y + term_z) + potential * wide


def ritz(correlation, hamil):
    scale = jnp.max(jnp.sum(jnp.abs(correlation), axis=1))
    current = correlation / scale
    identity = jnp.eye(correlation.shape[0], dtype=jnp.float32)
    inverse_root = identity
    for turn_index in range(NS_ITERS):
        turn = 1.5 * identity - 0.5 * jnp.dot(inverse_root, current, precision=lax.Precision.HIGHEST)
        current = jnp.dot(current, turn, precision=lax.Precision.HIGHEST)
        inverse_root = jnp.dot(turn, inverse_root, precision=lax.Precision.HIGHEST)
    projected = jnp.dot(jnp.dot(inverse_root.T, hamil, precision=lax.Precision.HIGHEST), inverse_root, precision=lax.Precision.HIGHEST) / scale
    return inverse_root.astype(jnp.bfloat16), projected


def reference(orbitals, potential):
    k_x = second_derivative(NX)
    k_y = second_derivative(NY)
    k_z = second_derivative(NZ)

    def filter_one(start):
        start_f = start.astype(jnp.float32)
        first = ((apply_ham(start, potential, k_x, k_y, k_z) - CENTER * start_f) / HALF_WIDTH).astype(jnp.bfloat16)
        first_f = first.astype(jnp.float32)
        filtered = (2.0 * (apply_ham(first, potential, k_x, k_y, k_z) - CENTER * first_f) / HALF_WIDTH - start_f).astype(jnp.bfloat16)
        applied = apply_ham(filtered, potential, k_x, k_y, k_z).astype(jnp.bfloat16)
        return filtered, applied

    filtered, applied = lax.map(filter_one, orbitals)
    flat = filtered.reshape(NB, -1)
    hflat = applied.reshape(NB, -1)
    correlation = jnp.dot(flat, flat.T, preferred_element_type=jnp.float32)
    hamil = jnp.dot(hflat, flat.T, preferred_element_type=jnp.float32)
    coeff, projected = ritz(correlation, hamil)
    rotated = jnp.dot(coeff.T, flat, preferred_element_type=jnp.float32).astype(jnp.bfloat16)
    return rotated.reshape(NB, NX, NY, NZ), projected
```

```python
import functools
import math

import jax
import jax.numpy as jnp
from jax import lax
from jax.experimental import pallas as pl
from jax.experimental.pallas import tpu as pltpu
from jax.sharding import PartitionSpec as P

NS_ITERS = 6


CENTER = 9.5
HALF_WIDTH = 6.5


def second_derivative(length):
    index = jnp.arange(length, dtype=jnp.int32)
    product = index[:, None] * index[None, :] % length
    angles = product.astype(jnp.float32) * (2.0 * math.pi / length)
    freq = jnp.minimum(index, length - index).astype(jnp.float32)
    weight = -((2.0 * math.pi / length * freq) ** 2) / length
    cosines = jnp.cos(angles)
    sines = jnp.sin(angles)
    matrix = jnp.dot(cosines * weight[None, :], cosines.T, precision=lax.Precision.HIGHEST)
    matrix = matrix + jnp.dot(sines * weight[None, :], sines.T, precision=lax.Precision.HIGHEST)
    return matrix.astype(jnp.bfloat16)


def plane_kernel(mode, field_ref, term_ref, potential_ref, ky_ref, kz_ref, *rest):
    out_ref = rest[-1]
    blocks, planes, rows, depth = field_ref.shape
    for plane in range(planes):
        field = field_ref[:, plane].reshape(blocks * rows, depth)
        wide = field.astype(jnp.float32)
        term_y = jnp.dot(ky_ref[...], field, preferred_element_type=jnp.float32)
        term_z = jnp.dot(field, kz_ref[...], preferred_element_type=jnp.float32)
        term_x = term_ref[:, plane].reshape(blocks * rows, depth).astype(jnp.float32)
        result = -0.5 * (term_x + term_y + term_z) + potential_ref[plane] * wide
        if mode == 1:
            result = (result - CENTER * wide) * (1.0 / HALF_WIDTH)
        elif mode == 2:
            start = rest[0][:, plane].reshape(blocks * rows, depth).astype(jnp.float32)
            result = (result - CENTER * wide) * (2.0 / HALF_WIDTH) - start
        out_ref[:, plane] = result.astype(jnp.bfloat16).reshape(blocks, rows, depth)


def plane_call(mode, field, term, potential, k_y, k_z, start=None):
    blocks, planes, rows, depth = field.shape
    step = 2
    tall = pl.BlockSpec((blocks, step, rows, depth), lambda i: (0, i, 0, 0))
    full = lambda k: pl.BlockSpec(k.shape, lambda i: (0, 0))
    operands = [field, term, potential, k_y, k_z]
    specs = [tall, tall, pl.BlockSpec((step,) + potential.shape[1:], lambda i: (i, 0, 0)), full(k_y), full(k_z)]
    if start is not None:
        operands.append(start)
        specs.append(tall)
    size = field.size
    return pl.pallas_call(
        functools.partial(plane_kernel, mode),
        grid=(planes // step,),
        in_specs=specs,
        out_specs=tall,
        out_shape=jax.ShapeDtypeStruct(field.shape, jnp.bfloat16),
        cost_estimate=pl.CostEstimate(
            flops=2 * size * (blocks * rows + depth), bytes_accessed=size * 12, transcendentals=0
        ),
    )(*operands)


def gram_kernel(count, *refs):
    left_refs, right_refs, out_ref = refs[:count], refs[count:-1], refs[-1]

    @pl.when(pl.program_id(0) == 0)
    def _():
        out_ref[...] = jnp.zeros_like(out_ref)

    bands, planes, rows, depth = left_refs[0].shape
    for plane in range(planes):
        pick = lambda group: jnp.concatenate(
            [ref[:, plane].reshape(bands * rows, depth) for ref in group], axis=0
        )
        right = pick(right_refs)
        left = right if left_refs is right_refs else pick(left_refs)
        out_ref[...] += lax.dot_general(
            left, right, (((1,), (1,)), ((), ())), preferred_element_type=jnp.float32
        )


def gram(left, right):
    count = len(left)
    bands, planes, rows, depth = left[0].shape
    step = 4
    side = count * bands * rows
    tall = pl.BlockSpec((bands, step, rows, depth), lambda i: (0, i, 0, 0))
    size = left[0].size * count
    wide = pl.pallas_call(
        functools.partial(gram_kernel, count),
        grid=(planes // step,),
        in_specs=[tall] * (2 * count),
        out_specs=pl.BlockSpec((side, side), lambda i: (0, 0)),
        out_shape=jax.ShapeDtypeStruct((side, side), jnp.float32),
        cost_estimate=pl.CostEstimate(
            flops=2 * size * side, bytes_accessed=size * 4, transcendentals=0
        ),
    )(*left, *right)
    wide = wide.reshape(count, bands, rows, count, bands, rows)
    same = jnp.eye(rows, dtype=jnp.float32)[None, None, :, None, None, :]
    small = jnp.sum(wide * same, axis=(2, 5))
    total = count * bands
    return small.transpose(1, 0, 3, 2).reshape(total, total)


def rotate_kernel(count, mix_ref, *refs):
    bands, planes, rows, depth = refs[0].shape
    part = bands * rows
    for plane in range(planes):
        fields = jnp.concatenate(
            [ref[:, plane].reshape(part, depth) for ref in refs[:count]], axis=0
        )
        mixed = jnp.dot(mix_ref[...], fields, preferred_element_type=jnp.float32)
        for slot in range(count):
            piece = mixed[slot * part : (slot + 1) * part].astype(jnp.bfloat16)
            refs[count + slot][:, plane] = piece.reshape(bands, rows, depth)


def rotate(coeff, fields):
    count = len(fields)
    bands, planes, rows, depth = fields[0].shape
    step = 4
    side = count * bands * rows
    ordered = coeff.reshape(bands, count, bands, count).transpose(3, 2, 1, 0)
    same = jnp.eye(rows, dtype=coeff.dtype)
    mix = (ordered[:, :, None, :, :, None] * same[None, None, :, None, None, :]).reshape(side, side)
    tall = pl.BlockSpec((bands, step, rows, depth), lambda i: (0, i, 0, 0))
    size = fields[0].size * count
    return pl.pallas_call(
        functools.partial(rotate_kernel, count),
        grid=(planes // step,),
        in_specs=[pl.BlockSpec((side, side), lambda i: (0, 0))] + [tall] * count,
        out_specs=[tall] * count,
        out_shape=[jax.ShapeDtypeStruct(fields[0].shape, jnp.bfloat16)] * count,
        cost_estimate=pl.CostEstimate(
            flops=2 * size * side, bytes_accessed=size * 4, transcendentals=0
        ),
    )(mix, *fields)


def ritz(correlation, hamil):
    scale = jnp.max(jnp.sum(jnp.abs(correlation), axis=1))
    current = correlation / scale
    identity = jnp.eye(correlation.shape[0], dtype=jnp.float32)
    inverse_root = identity
    for turn_index in range(NS_ITERS):
        turn = 1.5 * identity - 0.5 * jnp.dot(
            inverse_root, current, precision=lax.Precision.HIGHEST
        )
        current = jnp.dot(current, turn, precision=lax.Precision.HIGHEST)
        inverse_root = jnp.dot(turn, inverse_root, precision=lax.Precision.HIGHEST)
    projected = (
        jnp.dot(
            jnp.dot(inverse_root.T, hamil, precision=lax.Precision.HIGHEST),
            inverse_root,
            precision=lax.Precision.HIGHEST,
        )
        / scale
    )
    return (inverse_root.astype(jnp.bfloat16), projected)


def derive_x(field, k_x):
    blocks, planes, rows, depth = field.shape
    lines = lax.all_to_all(field, "grid", split_axis=0, concat_axis=0, tiled=True)
    derived = jnp.einsum(
        "jyz,jx->xyz",
        lines.reshape(blocks * planes, rows, depth),
        k_x,
        preferred_element_type=jnp.float32,
    ).astype(jnp.bfloat16)
    return lax.all_to_all(
        derived.reshape(field.shape), "grid", split_axis=0, concat_axis=0, tiled=True
    )


def swap_bands(field):
    return lax.all_to_all(field, "band", split_axis=0, concat_axis=0, tiled=True)


def per_device(orbitals, potential):
    own, planes, height, depth = orbitals.shape
    blocks = lax.axis_size("grid")
    bands = lax.axis_size("band")
    rows = height // blocks
    k_x = second_derivative(planes * blocks)
    k_y = second_derivative(height)
    k_z = second_derivative(depth)
    starts = [
        orbitals[o].reshape(planes, blocks, rows, depth).transpose(1, 0, 2, 3) for o in range(own)
    ]
    firsts = [plane_call(1, v, derive_x(v, k_x), potential, k_y.T, k_z) for v in starts]
    filtered = [
        plane_call(2, v, derive_x(v, k_x), potential, k_y.T, k_z, start)
        for v, start in zip(firsts, starts)
    ]
    applied = [plane_call(3, v, derive_x(v, k_x), potential, k_y.T, k_z) for v in filtered]
    shape = (bands, blocks // bands * planes, rows, depth)
    mixed_f = [swap_bands(v).reshape(shape) for v in filtered]
    mixed_h = [swap_bands(v).reshape(shape) for v in applied]
    correlation = lax.psum(gram(mixed_f, mixed_f), ("band", "grid"))
    hamil = lax.psum(gram(mixed_h, mixed_f), ("band", "grid"))
    coeff, projected = ritz(correlation, hamil)
    turned = rotate(coeff, mixed_f)
    back = [
        swap_bands(v.reshape(blocks, planes, rows, depth)).transpose(1, 0, 2, 3).reshape(
            planes, height, depth
        )
        for v in turned
    ]
    return (jnp.stack(back), projected)


def solution(mesh):
    in_specs = (P("band", "grid", None, None), P("grid", None, None))
    out_specs = (P("band", "grid", None, None), P())
    return jax.shard_map(
        per_device, mesh=mesh, in_specs=in_specs, out_specs=out_specs, check_vma=False
    )
```

```python
import functools
import math

import jax
import jax.numpy as jnp
from jax import lax
from jax.experimental import pallas as pl
from jax.experimental.pallas import tpu as pltpu
from jax.sharding import PartitionSpec as P

NS_ITERS = 6


CENTER = 9.5
HALF_WIDTH = 6.5


def second_derivative(length):
    index = jnp.arange(length, dtype=jnp.int32)
    product = index[:, None] * index[None, :] % length
    angles = product.astype(jnp.float32) * (2.0 * math.pi / length)
    freq = jnp.minimum(index, length - index).astype(jnp.float32)
    weight = -((2.0 * math.pi / length * freq) ** 2) / length
    cosines = jnp.cos(angles)
    sines = jnp.sin(angles)
    matrix = jnp.dot(cosines * weight[None, :], cosines.T, precision=lax.Precision.HIGHEST)
    matrix = matrix + jnp.dot(sines * weight[None, :], sines.T, precision=lax.Precision.HIGHEST)
    return matrix.astype(jnp.bfloat16)


def plane_kernel(mode, field_ref, term_ref, potential_ref, ky_ref, kz_ref, *rest):
    out_ref = rest[-1]
    blocks, planes, rows, depth = field_ref.shape
    for plane in range(planes):
        field = field_ref[:, plane].reshape(blocks * rows, depth)
        wide = field.astype(jnp.float32)
        term_y = jnp.dot(ky_ref[...], field, preferred_element_type=jnp.float32)
        term_z = jnp.dot(field, kz_ref[...], preferred_element_type=jnp.float32)
        term_x = term_ref[:, plane].reshape(blocks * rows, depth).astype(jnp.float32)
        result = -0.5 * (term_x + term_y + term_z) + potential_ref[plane] * wide
        if mode == 1:
            result = (result - CENTER * wide) * (1.0 / HALF_WIDTH)
        elif mode == 2:
            start = rest[0][:, plane].reshape(blocks * rows, depth).astype(jnp.float32)
            result = (result - CENTER * wide) * (2.0 / HALF_WIDTH) - start
        out_ref[:, plane] = result.astype(jnp.bfloat16).reshape(blocks, rows, depth)


def plane_call(mode, field, term, potential, k_y, k_z, start=None):
    blocks, planes, rows, depth = field.shape
    step = 2
    tall = pl.BlockSpec((blocks, step, rows, depth), lambda i: (0, i, 0, 0))
    full = lambda k: pl.BlockSpec(k.shape, lambda i: (0, 0))
    operands = [field, term, potential, k_y, k_z]
    specs = [tall, tall, pl.BlockSpec((step,) + potential.shape[1:], lambda i: (i, 0, 0)), full(k_y), full(k_z)]
    if start is not None:
        operands.append(start)
        specs.append(tall)
    size = field.size
    return pl.pallas_call(
        functools.partial(plane_kernel, mode),
        grid=(planes // step,),
        in_specs=specs,
        out_specs=tall,
        out_shape=jax.ShapeDtypeStruct(field.shape, jnp.bfloat16),
        cost_estimate=pl.CostEstimate(
            flops=2 * size * (blocks * rows + depth), bytes_accessed=size * 12, transcendentals=0
        ),
    )(*operands)


def stack_rows(refs, plane):
    return jnp.concatenate([ref[plane] for ref in refs], axis=0)


def gram_kernel(left_count, *refs):
    left_refs, right_refs, out_ref = refs[:left_count], refs[left_count:-1], refs[-1]

    @pl.when(pl.program_id(0) == 0)
    def _():
        out_ref[...] = jnp.zeros_like(out_ref)

    for plane in range(refs[0].shape[0]):
        right = stack_rows(right_refs, plane)
        left = stack_rows(left_refs, plane) if left_count else right
        out_ref[...] += lax.dot_general(
            left, right, (((1,), (1,)), ((), ())), preferred_element_type=jnp.float32
        )


def gram(left, right):
    planes, rows, depth = right[0].shape
    step = math.gcd(planes, 8)
    tall = len(left or right) * rows
    wide = len(right) * rows
    piece = pl.BlockSpec((step, rows, depth), lambda i: (i, 0, 0))
    size = planes * rows * depth
    products = pl.pallas_call(
        functools.partial(gram_kernel, len(left)),
        grid=(planes // step,),
        in_specs=[piece] * (len(left) + len(right)),
        out_specs=pl.BlockSpec((tall, wide), lambda i: (0, 0)),
        out_shape=jax.ShapeDtypeStruct((tall, wide), jnp.float32),
        cost_estimate=pl.CostEstimate(
            flops=2 * planes * depth * tall * wide,
            bytes_accessed=2 * size * (len(left) + len(right)),
            transcendentals=0,
        ),
    )(*left, *right)
    products = products.reshape(tall // rows, rows, wide // rows, rows)
    same = jnp.eye(rows, dtype=jnp.float32)[None, :, None, :]
    return jnp.sum(products * same, axis=(1, 3))


def rotate_kernel(count, mix_ref, *refs):
    planes, rows, depth = refs[0].shape
    for plane in range(planes):
        mixed = jnp.dot(
            mix_ref[...], stack_rows(refs[:count], plane), preferred_element_type=jnp.float32
        ).astype(jnp.bfloat16)
        for slot in range(count):
            refs[count + slot][plane] = mixed[slot * rows : (slot + 1) * rows]


def rotate(coeff, pieces):
    count = len(pieces)
    planes, rows, depth = pieces[0].shape
    step = math.gcd(planes, 8)
    side = count * rows
    same = jnp.eye(rows, dtype=coeff.dtype)
    mix = (coeff.T[:, None, :, None] * same[None, :, None, :]).reshape(side, side)
    piece = pl.BlockSpec((step, rows, depth), lambda i: (i, 0, 0))
    return pl.pallas_call(
        functools.partial(rotate_kernel, count),
        grid=(planes // step,),
        in_specs=[pl.BlockSpec((side, side), lambda i: (0, 0))] + [piece] * count,
        out_specs=[piece] * count,
        out_shape=[jax.ShapeDtypeStruct(pieces[0].shape, jnp.bfloat16)] * count,
        cost_estimate=pl.CostEstimate(
            flops=2 * planes * depth * side * side,
            bytes_accessed=4 * planes * depth * side,
            transcendentals=0,
        ),
    )(mix, *pieces)


def ritz(correlation, hamil):
    scale = jnp.max(jnp.sum(jnp.abs(correlation), axis=1))
    current = correlation / scale
    identity = jnp.eye(correlation.shape[0], dtype=jnp.float32)
    inverse_root = identity
    for turn_index in range(NS_ITERS):
        turn = 1.5 * identity - 0.5 * jnp.dot(
            inverse_root, current, precision=lax.Precision.HIGHEST
        )
        current = jnp.dot(current, turn, precision=lax.Precision.HIGHEST)
        inverse_root = jnp.dot(turn, inverse_root, precision=lax.Precision.HIGHEST)
    projected = (
        jnp.dot(
            jnp.dot(inverse_root.T, hamil, precision=lax.Precision.HIGHEST),
            inverse_root,
            precision=lax.Precision.HIGHEST,
        )
        / scale
    )
    return (inverse_root.astype(jnp.bfloat16), projected)


def along_x(lines, k_x):
    blocks, planes, rows, depth = lines.shape
    derived = jnp.einsum(
        "jyz,jx->xyz",
        lines.reshape(blocks * planes, rows, depth),
        k_x,
        preferred_element_type=jnp.float32,
    ).astype(jnp.bfloat16)
    return derived.reshape(lines.shape)


def exchange(field):
    return lax.all_to_all(field, "grid", split_axis=0, concat_axis=0, tiled=True)


def derive_x(field, k_x):
    return exchange(along_x(exchange(field), k_x))


def shift_bands(piece, bands, step):
    return lax.ppermute(piece, "band", [(b, (b + step) % bands) for b in range(bands)])


def chunk_of(field, bands, step):
    width = field.shape[0] // bands
    where = lax.rem(lax.axis_index("band") + step, bands)
    chunk = lax.dynamic_slice_in_dim(field, where * width, width, 0)
    return chunk.reshape((-1,) + field.shape[2:])


def reorder(matrix, pick, axis):
    moved = jnp.moveaxis(matrix, axis, 0)
    mask = pick.reshape(pick.shape + (1,) * (moved.ndim - 1))
    return jnp.moveaxis(jnp.sum(jnp.where(mask, moved[None], 0), axis=1), 0, axis)


def per_device(orbitals, potential):
    own, planes, height, depth = orbitals.shape
    blocks = lax.axis_size("grid")
    bands = lax.axis_size("band")
    total = own * bands
    rows = height // blocks
    k_x = second_derivative(planes * blocks)
    k_y = second_derivative(height)
    k_z = second_derivative(depth)
    starts = [
        orbitals[o].reshape(planes, blocks, rows, depth).transpose(1, 0, 2, 3) for o in range(own)
    ]
    firsts = [plane_call(1, v, derive_x(v, k_x), potential, k_y.T, k_z) for v in starts]
    filtered = [
        plane_call(2, v, derive_x(v, k_x), potential, k_y.T, k_z, start)
        for v, start in zip(firsts, starts)
    ]
    odd, even = range(1, bands, 2), range(2, bands, 2)
    chunks_f = [[chunk_of(v, bands, k) for k in range(bands)] for v in filtered]
    moved_f = [[group[0]] + [None] * (bands - 1) for group in chunks_f]

    def beside(window, number):
        slot, steps = number // 2, (odd, even)[number % 2]
        moving = [shift_bands(chunks_f[slot][k], bands, k) for k in steps]
        window, moving = lax.optimization_barrier((window, moving))
        for k, piece in zip(steps, moving):
            moved_f[slot][k] = piece
        return window

    lines = [beside(exchange(v), o) for o, v in enumerate(filtered)]
    derived = [along_x(v, k_x) for v in lines]
    terms = [beside(exchange(v), own + o) for o, v in enumerate(derived)]
    pieces_f = [piece for group in moved_f for piece in group]
    applied = [plane_call(3, v, t, potential, k_y.T, k_z) for v, t in zip(filtered, terms)]
    absent = bands // 2 if bands % 2 == 0 else bands
    chunks_h = [[chunk_of(v, bands, k) for k in range(bands)] for v in applied]
    pieces_h = [
        shift_bands(group[k], bands, k) if k else group[k]
        for group in chunks_h
        for k in range(bands)
        if k != absent
    ]

    def hamil_part():
        part = gram(pieces_h, pieces_f)
        if absent == bands:
            return part
        kept = bands - 1
        part = part.reshape(own, kept, total)
        gap = jnp.zeros((own, 1, total), jnp.float32)
        part = jnp.concatenate([part[:, :absent], gap, part[:, absent:]], axis=1)
        part = part.reshape(total, total)
        hole = (jnp.arange(total) % bands == absent)[:, None]
        part = jnp.where(hole, part.T, part)
        local = gram([g[absent] for g in chunks_h], [g[absent] for g in chunks_f])
        home = jnp.arange(total) % bands == 0
        local = jnp.repeat(jnp.repeat(local, bands, axis=0), bands, axis=1)
        return part + jnp.where(home[:, None] & home[None, :], local, 0.0)

    me = lax.axis_index("band")
    steps = jnp.arange(bands, dtype=jnp.int32)
    source = (me - steps + bands) % bands
    target = (me + steps) % bands
    by_band = steps[:, None] == source[None, :]
    to_source = source[:, None] == steps[None, :]
    to_target = target[:, None] == steps[None, :]

    def in_order(matrix):
        matrix = matrix.reshape(own, bands, own, bands)
        matrix = reorder(reorder(matrix, by_band, 1), by_band, 3)
        return matrix.transpose(1, 0, 3, 2).reshape(total, total)

    correlation = lax.psum(in_order(gram([], pieces_f)), ("band", "grid"))
    mine, correlation = lax.optimization_barrier(
        (in_order(hamil_part()), correlation)
    )
    hamil = lax.psum(mine, ("band", "grid"))
    coeff, projected = ritz(correlation, hamil)
    ordered = coeff.reshape(bands, own, bands, own).transpose(1, 0, 3, 2)
    ordered = reorder(reorder(ordered, to_source, 1), to_target, 3).reshape(total, total)
    turned = rotate(ordered, pieces_f)

    rotated = jnp.zeros(orbitals.shape, jnp.bfloat16)
    width = blocks // bands
    for o in range(own):
        for k in range(bands):
            piece = turned[o * bands + k]
            piece = shift_bands(piece, bands, k) if k else piece
            lines = piece.reshape(width, planes, rows, depth).transpose(1, 0, 2, 3)
            rotated = lax.dynamic_update_slice(
                rotated,
                lines.reshape(1, planes, width * rows, depth),
                (o, 0, source[k] * (width * rows), 0),
            )
    return (rotated, projected)


def solution(mesh):
    in_specs = (P("band", "grid", None, None), P("grid", None, None))
    out_specs = (P("band", "grid", None, None), P())
    return jax.shard_map(
        per_device, mesh=mesh, in_specs=in_specs, out_specs=out_specs, check_vma=False
    )
```

```python
import functools
import math

import jax
import jax.numpy as jnp
from jax import lax
from jax.experimental import pallas as pl
from jax.experimental.pallas import tpu as pltpu
from jax.sharding import PartitionSpec as P

NS_ITERS = 6


CENTER = 9.5
HALF_WIDTH = 6.5


def second_derivative(length):
    index = jnp.arange(length, dtype=jnp.int32)
    product = index[:, None] * index[None, :] % length
    angles = product.astype(jnp.float32) * (2.0 * math.pi / length)
    freq = jnp.minimum(index, length - index).astype(jnp.float32)
    weight = -((2.0 * math.pi / length * freq) ** 2) / length
    cosines = jnp.cos(angles)
    sines = jnp.sin(angles)
    matrix = jnp.dot(cosines * weight[None, :], cosines.T, precision=lax.Precision.HIGHEST)
    matrix = matrix + jnp.dot(sines * weight[None, :], sines.T, precision=lax.Precision.HIGHEST)
    return matrix.astype(jnp.bfloat16)


def plane_kernel(mode, field_ref, term_ref, potential_ref, ky_ref, kz_ref, *rest):
    out_ref = rest[-1]
    blocks, planes, rows, depth = field_ref.shape
    for plane in range(planes):
        field = field_ref[:, plane].reshape(blocks * rows, depth)
        wide = field.astype(jnp.float32)
        term_y = jnp.dot(ky_ref[...], field, preferred_element_type=jnp.float32)
        term_z = jnp.dot(field, kz_ref[...], preferred_element_type=jnp.float32)
        term_x = term_ref[:, plane].reshape(blocks * rows, depth).astype(jnp.float32)
        result = -0.5 * (term_x + term_y + term_z) + potential_ref[plane] * wide
        if mode == 1:
            result = (result - CENTER * wide) * (1.0 / HALF_WIDTH)
        elif mode == 2:
            start = rest[0][:, plane].reshape(blocks * rows, depth).astype(jnp.float32)
            result = (result - CENTER * wide) * (2.0 / HALF_WIDTH) - start
        out_ref[:, plane] = result.astype(jnp.bfloat16).reshape(blocks, rows, depth)


def plane_call(mode, field, term, potential, k_y, k_z, start=None):
    blocks, planes, rows, depth = field.shape
    step = 2
    tall = pl.BlockSpec((blocks, step, rows, depth), lambda i: (0, i, 0, 0))
    full = lambda k: pl.BlockSpec(k.shape, lambda i: (0, 0))
    operands = [field, term, potential, k_y, k_z]
    specs = [tall, tall, pl.BlockSpec((step,) + potential.shape[1:], lambda i: (i, 0, 0)), full(k_y), full(k_z)]
    if start is not None:
        operands.append(start)
        specs.append(tall)
    size = field.size
    return pl.pallas_call(
        functools.partial(plane_kernel, mode),
        grid=(planes // step,),
        in_specs=specs,
        out_specs=tall,
        out_shape=jax.ShapeDtypeStruct(field.shape, jnp.bfloat16),
        cost_estimate=pl.CostEstimate(
            flops=2 * size * (blocks * rows + depth), bytes_accessed=size * 12, transcendentals=0
        ),
    )(*operands)


def stack_rows(refs, plane):
    return jnp.concatenate([ref[plane] for ref in refs], axis=0)


def gram_kernel(left_count, *refs):
    left_refs, right_refs, out_ref = refs[:left_count], refs[left_count:-1], refs[-1]

    @pl.when(pl.program_id(0) == 0)
    def _():
        out_ref[...] = jnp.zeros_like(out_ref)

    for plane in range(refs[0].shape[0]):
        right = stack_rows(right_refs, plane)
        left = stack_rows(left_refs, plane) if left_count else right
        out_ref[...] += lax.dot_general(
            left, right, (((1,), (1,)), ((), ())), preferred_element_type=jnp.float32
        )


def gram(left, right):
    planes, rows, depth = right[0].shape
    step = math.gcd(planes, 4)
    tall = len(left or right) * rows
    wide = len(right) * rows
    piece = pl.BlockSpec((step, rows, depth), lambda i: (i, 0, 0))
    size = planes * rows * depth
    products = pl.pallas_call(
        functools.partial(gram_kernel, len(left)),
        grid=(planes // step,),
        in_specs=[piece] * (len(left) + len(right)),
        out_specs=pl.BlockSpec((tall, wide), lambda i: (0, 0)),
        out_shape=jax.ShapeDtypeStruct((tall, wide), jnp.float32),
        cost_estimate=pl.CostEstimate(
            flops=2 * planes * depth * tall * wide,
            bytes_accessed=2 * size * (len(left) + len(right)),
            transcendentals=0,
        ),
    )(*left, *right)
    products = products.reshape(tall // rows, rows, wide // rows, rows)
    same = jnp.eye(rows, dtype=jnp.float32)[None, :, None, :]
    return jnp.sum(products * same, axis=(1, 3))


def rotate_kernel(count, mix_ref, *refs):
    planes, rows, depth = refs[0].shape
    for plane in range(planes):
        mixed = jnp.dot(
            mix_ref[...], stack_rows(refs[:count], plane), preferred_element_type=jnp.float32
        ).astype(jnp.bfloat16)
        for slot in range(count):
            refs[count + slot][plane] = mixed[slot * rows : (slot + 1) * rows]


def rotate(coeff, pieces):
    count = len(pieces)
    planes, rows, depth = pieces[0].shape
    step = math.gcd(planes, 4)
    side = count * rows
    same = jnp.eye(rows, dtype=coeff.dtype)
    mix = (coeff.T[:, None, :, None] * same[None, :, None, :]).reshape(side, side)
    piece = pl.BlockSpec((step, rows, depth), lambda i: (i, 0, 0))
    return pl.pallas_call(
        functools.partial(rotate_kernel, count),
        grid=(planes // step,),
        in_specs=[pl.BlockSpec((side, side), lambda i: (0, 0))] + [piece] * count,
        out_specs=[piece] * count,
        out_shape=[jax.ShapeDtypeStruct(pieces[0].shape, jnp.bfloat16)] * count,
        cost_estimate=pl.CostEstimate(
            flops=2 * planes * depth * side * side,
            bytes_accessed=4 * planes * depth * side,
            transcendentals=0,
        ),
    )(mix, *pieces)


def inverse_root_of(correlation):
    scale = jnp.max(jnp.sum(jnp.abs(correlation), axis=1))
    current = correlation / scale
    identity = jnp.eye(correlation.shape[0], dtype=jnp.float32)
    inverse_root = identity
    for turn_index in range(NS_ITERS):
        turn = 1.5 * identity - 0.5 * jnp.dot(
            inverse_root, current, precision=lax.Precision.HIGHEST
        )
        current = jnp.dot(current, turn, precision=lax.Precision.HIGHEST)
        inverse_root = jnp.dot(turn, inverse_root, precision=lax.Precision.HIGHEST)
    return scale, inverse_root


def project(hamil, scale, inverse_root):
    return (
        jnp.dot(
            jnp.dot(inverse_root.T, hamil, precision=lax.Precision.HIGHEST),
            inverse_root,
            precision=lax.Precision.HIGHEST,
        )
        / scale
    )


def sum_all(value):
    sizes = {axis: lax.axis_size(axis) for axis in ("grid", "band")}
    if any(n & (n - 1) for n in sizes.values()):
        return lax.psum(value, ("band", "grid"))
    for axis, n in sizes.items():
        bit = 1
        while bit < n:
            value = value + lax.ppermute(value, axis, [(i, i ^ bit) for i in range(n)])
            bit *= 2
    return value


def along_x(lines, k_x):
    blocks, planes, rows, depth = lines.shape
    derived = jnp.einsum(
        "jyz,jx->xyz",
        lines.reshape(blocks * planes, rows, depth),
        k_x,
        preferred_element_type=jnp.float32,
    ).astype(jnp.bfloat16)
    return derived.reshape(lines.shape)


def exchange(field):
    return lax.all_to_all(field, "grid", split_axis=0, concat_axis=0, tiled=True)


def derive_x(field, k_x):
    return exchange(along_x(exchange(field), k_x))


def shift_bands(piece, bands, step):
    return lax.ppermute(piece, "band", [(b, (b + step) % bands) for b in range(bands)])


def chunk_of(field, bands, step):
    width = field.shape[0] // bands
    where = lax.rem(lax.axis_index("band") + step, bands)
    chunk = lax.dynamic_slice_in_dim(field, where * width, width, 0)
    return chunk.reshape((-1,) + field.shape[2:])


def reorder(matrix, pick, axis):
    moved = jnp.moveaxis(matrix, axis, 0)
    mask = pick.reshape(pick.shape + (1,) * (moved.ndim - 1))
    return jnp.moveaxis(jnp.sum(jnp.where(mask, moved[None], 0), axis=1), 0, axis)


def per_device(orbitals, potential):
    own, planes, height, depth = orbitals.shape
    blocks = lax.axis_size("grid")
    bands = lax.axis_size("band")
    total = own * bands
    rows = height // blocks
    k_x = second_derivative(planes * blocks)
    k_y = second_derivative(height)
    k_z = second_derivative(depth)
    starts = [
        orbitals[o].reshape(planes, blocks, rows, depth).transpose(1, 0, 2, 3) for o in range(own)
    ]
    firsts = [plane_call(1, v, derive_x(v, k_x), potential, k_y.T, k_z) for v in starts]
    filtered = [
        plane_call(2, v, derive_x(v, k_x), potential, k_y.T, k_z, start)
        for v, start in zip(firsts, starts)
    ]
    odd, even = range(1, bands, 2), range(2, bands, 2)
    chunks_f = [[chunk_of(v, bands, k) for k in range(bands)] for v in filtered]
    moved_f = [[group[0]] + [None] * (bands - 1) for group in chunks_f]

    def beside(window, number):
        slot, steps = number // 2, (odd, even)[number % 2]
        moving = [shift_bands(chunks_f[slot][k], bands, k) for k in steps]
        window, moving = lax.optimization_barrier((window, moving))
        for k, piece in zip(steps, moving):
            moved_f[slot][k] = piece
        return window

    lines = [beside(exchange(v), o) for o, v in enumerate(filtered)]
    derived = [along_x(v, k_x) for v in lines]
    terms = [beside(exchange(v), own + o) for o, v in enumerate(derived)]
    pieces_f = [piece for group in moved_f for piece in group]
    applied = [plane_call(3, v, t, potential, k_y.T, k_z) for v, t in zip(filtered, terms)]
    pieces_h = []
    for v in applied:
        pieces_h.append(chunk_of(v, bands, 0))
        pieces_h += [shift_bands(chunk_of(v, bands, k), bands, k) for k in range(1, bands)]

    me = lax.axis_index("band")
    steps = jnp.arange(bands, dtype=jnp.int32)
    source = (me - steps + bands) % bands
    target = (me + steps) % bands
    by_band = steps[:, None] == source[None, :]
    to_source = source[:, None] == steps[None, :]
    to_target = target[:, None] == steps[None, :]

    def in_order(matrix):
        matrix = matrix.reshape(own, bands, own, bands)
        matrix = reorder(reorder(matrix, by_band, 1), by_band, 3)
        return matrix.transpose(1, 0, 3, 2).reshape(total, total)

    correlation = sum_all(in_order(gram([], pieces_f)))
    scale, inverse_root = inverse_root_of(correlation)
    coeff = inverse_root.astype(jnp.bfloat16)
    ordered = coeff.reshape(bands, own, bands, own).transpose(1, 0, 3, 2)
    ordered = reorder(reorder(ordered, to_source, 1), to_target, 3).reshape(total, total)
    turned = rotate(ordered, pieces_f)
    pieces_h, _ = lax.optimization_barrier((pieces_h, turned[0]))
    hamil = sum_all(in_order(gram(pieces_h, pieces_f)))
    projected = project(hamil, scale, inverse_root)

    rotated = jnp.zeros(orbitals.shape, jnp.bfloat16)
    width = blocks // bands
    for o in range(own):
        for k in range(bands):
            piece = turned[o * bands + k]
            piece = shift_bands(piece, bands, k) if k else piece
            lines = piece.reshape(width, planes, rows, depth).transpose(1, 0, 2, 3)
            rotated = lax.dynamic_update_slice(
                rotated,
                lines.reshape(1, planes, width * rows, depth),
                (o, 0, source[k] * (width * rows), 0),
            )
    return (rotated, projected)


def solution(mesh):
    in_specs = (P("band", "grid", None, None), P("grid", None, None))
    out_specs = (P("band", "grid", None, None), P())
    return jax.shard_map(
        per_device, mesh=mesh, in_specs=in_specs, out_specs=out_specs, check_vma=False
    )
```
